32 devices in a mesh: section: 4 (over y, x), tp: 8 (over z, core).
Axes of the slice: x: 2, y: 2, z: 4, core: 2. Of those that a mesh axis runs over, the one named last changes fastest.
Arguments:
- entering: bfloat16 [2, 3, 32, 4096], P(None, None, None, 'tp'), may hold values from -6 to 6
- output_grad: bfloat16 [2, 3, 32, 4096], P(None, None, None, 'tp'), may hold values from -6 to 6
- live_counts: int32 [2, 3], replicated, may hold values from 1 to 32, as said below
- segment_ids: int32 [2, 3, 32], replicated, may hold values from 0 to 3, never falling along the last dimension, each value on 1 to 16 neighbouring positions
- weight_in: bfloat16 [4, 4096, 11008], P('section', None, 'tp'), may hold values from -0.125 to 0.125
- weight_out: bfloat16 [4, 11008, 4096], P('section', 'tp'), may hold values from -0.078125 to 0.078125
- norm_gain: bfloat16 [4, 4096], P('section'), may hold values from 0.25 to 1.75
- shift_mix: bfloat16 [4, 4096], P('section'), may hold values from 0.099609375 to 0.8984375
Outputs:
- grad_in: bfloat16 [4, 4096, 11008], P('section', None, 'tp')
- grad_out: bfloat16 [4, 11008, 4096], P('section', 'tp')
- grad_gain: float32 [4, 4096], P('section', 'tp')
- grad_mix: float32 [4, 4096], P('section', 'tp')
The draws below stay inside these ranges and needn't reach their ends.
Inputs may be any that keep to these rules, and one draw needn't show every extreme that they name: `live_counts`: in each relay at least one micro-batch has all 32 rows live. `segment_ids`: never falls along the rows of a micro-batch.
All inputs are finite; a program needn't handle non-finite values.
Results may differ from the reference program's by a relative error of at most 0.03.
Values may be sent and summed in bfloat16 or wider, within the bound.
A program may use at most 256 MiB of HBM per device.

```python
import math
import jax
import jax.numpy as jnp
import numpy as np
from jax import lax

D = 4096
FF = 11008
TOK = 32
MB = 3
LAYERS = 4
N_TP = 8


def draw_live_counts(key, part):
    key_counts, key_choice = jax.random.split(key)
    counts = jax.random.randint(key_counts, (2, MB), TOK // 4, TOK + 1)
    chosen = jax.random.randint(key_choice, (2, 1), 0, MB)
    slot_ids = jnp.arange(MB)[None, :]
    return jnp.where(slot_ids == chosen, TOK, counts).astype(jnp.int32)


def spiked(array, key, source, target, parts, factor):
    def block_of(dim):
        return (jnp.arange(array.shape[dim]) // (array.shape[dim] // parts)).reshape((-1,) + (1,) * (array.ndim - 1 - dim))

    first = jax.random.permutation(key, parts)[block_of(target)]
    other_side = (block_of(target) + parts // 2) % parts
    return jnp.where((block_of(source) == first) | (block_of(source) == other_side), factor * array, array)


def block_scale(own_key, extent, cuts, least, largest):
    factor_of = 1.0
    for position, parts in cuts:
        steps = jax.random.uniform(jax.random.fold_in(jax.random.fold_in(own_key, 6), position), (parts,), jnp.float32, least / len(cuts), largest / len(cuts))
        factor_of = factor_of * jnp.repeat(jnp.exp(steps), extent[position] // parts).reshape((-1,) + (1,) * (len(extent) - 1 - position))
    return factor_of


def profile(amount, total, bound, slope):
    portions = [(1 << 20) // math.isqrt(rank ** slope) + 1 for rank in range(2, amount + 1)]
    spare, given = total - bound - (amount - 1), [1] * (amount - 1)
    while spare > 0:
        free = [i for i in range(amount - 1) if given[i] < bound]
        whole, left = sum([portions[i] for i in free]), spare
        for i in free:
            extra = min(bound - given[i], max(1, left * portions[i] // whole), spare)
            given[i] = given[i] + extra
            spare = spare - extra
    return np.array([bound] + given)


def ragged_sizes(own_key, amount, total, limit, skew):
    if amount == 2:
        one = jax.random.randint(own_key, (), max(1, total - limit), min(limit, total - 1) + 1)
        return jnp.stack([one, total - one])
    lengths = jnp.asarray(profile(amount, total, limit, skew), jnp.int32)
    twos = (amount - 1) // 2
    donor, sink = lengths[1:1 + 2 * twos:2], lengths[2:2 + 2 * twos:2]
    room = jnp.minimum(donor - 1, limit - sink)
    moved = jax.random.randint(jax.random.fold_in(own_key, 1), (twos,), 0, 1 << 20) % (room + 1)
    lengths = lengths.at[1:1 + 2 * twos:2].set(donor - moved).at[2:2 + 2 * twos:2].set(sink + moved)
    return lengths[jax.random.permutation(jax.random.fold_in(own_key, 2), amount)]


def normal_values(rng, shape, scale, bound, cuts=(), kind=jnp.bfloat16):
    drawn = jax.random.normal(rng, shape, jnp.float32) * scale
    if len(cuts) > 0:
        drawn = block_scale(rng, shape, cuts, -0.22, 0.18) * drawn
    return jnp.clip(drawn, min=-bound, max=bound).astype(kind)


def noise_with(rng, extent, spread, reach, cuts, heavy, dtype=jnp.bfloat16):
    array = spread * jax.random.normal(rng, extent, jnp.float32)
    if cuts:
        array = array * block_scale(rng, extent, cuts, -0.22, 0.18)
    return jnp.clip(spiked(array, jax.random.fold_in(rng, 3), *heavy), -reach, reach).astype(dtype)


def setup_inputs(seed: int = 0) -> dict:
    streams_of = jax.random.split(jax.random.key(seed), 9)
    entering = normal_values(streams_of[0], (2, MB, TOK, D), 1.0, 6.0, ((3, 8),))
    output_grad = normal_values(streams_of[1], (2, MB, TOK, D), 1.0, 6.0, ((3, 8),))
    live_counts = draw_live_counts(jax.random.fold_in(streams_of[8], 71), 0)
    segment_ids = jax.vmap(lambda own: jnp.searchsorted(jnp.cumsum(ragged_sizes(own, 4, TOK, TOK // 2, 1)), jnp.arange(TOK), side="right"))(jax.random.split(streams_of[3], 2 * MB)).reshape((2, MB, TOK)).astype(jnp.int32)
    weight_in = noise_with(streams_of[4], (LAYERS, D, FF), D ** -0.5, 0.125, ((0, 4), (2, 8)), (2, 1, 8, 2.0))
    weight_out = noise_with(streams_of[5], (LAYERS, FF, D), FF ** -0.5, 0.078125, ((0, 4), (1, 8)), (1, 2, 8, 2.0))
    norm_gain = jnp.clip(1.0 + 0.15 * jax.random.normal(streams_of[6], (LAYERS, D), jnp.float32), 0.25, 1.75).astype(jnp.bfloat16)
    shift_mix = jnp.clip(0.099609375 + 0.7988281 * jax.random.uniform(streams_of[7], (LAYERS, D), jnp.float32) ** block_scale(streams_of[7], (LAYERS, D), ((0, 4),), -0.2, 0.2), 0.099609375, 0.8984375).astype(jnp.bfloat16)
    return {"entering": entering, "output_grad": output_grad, "live_counts": live_counts, "segment_ids": segment_ids, "weight_in": weight_in, "weight_out": weight_out, "norm_gain": norm_gain, "shift_mix": shift_mix}


epsilon = 1e-05

def row_linkage(segment_ids):
    joined = segment_ids[..., 1:] == segment_ids[..., :-1]
    leading = jnp.zeros(segment_ids.shape[:-1] + (1,), jnp.float32)
    return jnp.concatenate([leading, joined.astype(jnp.float32)], axis=-1)

def earlier_rows(values, linkage):
    shifted = jnp.concatenate([jnp.zeros_like(values[..., :1, :]), values[..., :-1, :]], axis=-2)
    return shifted * linkage[..., None]

def later_rows(values, linkage):
    shifted = values[..., 1:, :] * linkage[..., 1:, None]
    return jnp.concatenate([shifted, jnp.zeros_like(values[..., :1, :])], axis=-2)

def silu_slope(pre_act):
    sigmoid = jax.nn.sigmoid(pre_act)
    return sigmoid * (1.0 + pre_act * (1.0 - sigmoid))

def rounded(values):
    return lax.optimization_barrier(values.astype(jnp.bfloat16)).astype(jnp.float32)

def mixed_rows(inputs, linkage, mix_values):
    floats = inputs.astype(jnp.float32)
    earlier = earlier_rows(floats, linkage)
    return (floats, earlier, floats + mix_values * (earlier - floats))

def forward_pieces(inputs, linkage, gain_values, mix_values, first_weights):
    floats, earlier, united = mixed_rows(inputs, linkage, mix_values)
    squares = lax.optimization_barrier(jnp.sum(united * united, axis=-1))
    row_scale = lax.rsqrt(squares / D + epsilon)
    normed = (united * gain_values).astype(jnp.bfloat16)
    summed = jnp.einsum('pmtd,df->pmtf', normed.astype(jnp.float32), first_weights.astype(jnp.float32))
    pre_act = row_scale[..., None] * summed
    hidden = jax.nn.silu(pre_act).astype(jnp.bfloat16)
    return (floats, earlier, united, row_scale, normed, summed, pre_act, hidden)

def reference(entering, output_grad, live_counts, segment_ids, weight_in, weight_out, norm_gain, shift_mix):
    linkage = row_linkage(segment_ids)
    row_index = jnp.arange(TOK)
    live_rows = (row_index[None, None, :] < live_counts[..., None]).astype(jnp.float32)
    hidden_block = FF // N_TP
    layer_inputs = [entering]
    for layer_index in range(LAYERS):
        gain_values = norm_gain[layer_index].astype(jnp.float32)
        mix_values = shift_mix[layer_index].astype(jnp.float32)
        pieces = forward_pieces(layer_inputs[-1], linkage, gain_values, mix_values, weight_in[layer_index])
        floats, hidden = (pieces[0], pieces[7])
        blocks = hidden.astype(jnp.float32).reshape(hidden.shape[:-1] + (N_TP, hidden_block))
        out_weights = weight_out[layer_index].astype(jnp.float32).reshape(N_TP, hidden_block, D)
        partial_value = jnp.einsum('pmtjf,jfd->pmtjd', blocks, out_weights)
        added = lax.optimization_barrier(jnp.sum(rounded(partial_value), axis=3))
        layer_inputs.append((floats + added).astype(jnp.bfloat16))
    upstream = (output_grad.astype(jnp.float32) * live_rows[..., None]).astype(jnp.bfloat16)
    first_list, second_list, gain_list, mix_list = ([], [], [], [])
    for layer_index in reversed(range(LAYERS)):
        gain_values = norm_gain[layer_index].astype(jnp.float32)
        mix_values = shift_mix[layer_index].astype(jnp.float32)
        floats, earlier, united, row_scale, normed, summed, pre_act, hidden = forward_pieces(layer_inputs[layer_index], linkage, gain_values, mix_values, weight_in[layer_index])
        upstream_float = upstream.astype(jnp.float32)
        second_grad = jnp.einsum('pmtf,pmtd->pfd', hidden.astype(jnp.float32), upstream_float)
        grad_hidden = jnp.einsum('pmtd,fd->pmtf', upstream_float, weight_out[layer_index].astype(jnp.float32))
        gate_grad = grad_hidden * silu_slope(pre_act)
        grad_summed = (gate_grad * row_scale[..., None]).astype(jnp.bfloat16)
        grad_rate = lax.optimization_barrier(jnp.sum(gate_grad * summed, axis=-1))
        first_grad = jnp.einsum('pmtd,pmtf->pdf', normed.astype(jnp.float32), grad_summed.astype(jnp.float32))
        blocks = grad_summed.astype(jnp.float32).reshape(grad_summed.shape[:-1] + (N_TP, hidden_block))
        in_weights = weight_in[layer_index].astype(jnp.float32).reshape(D, N_TP, hidden_block)
        partial_value = jnp.einsum('pmtjf,djf->pmtjd', blocks, in_weights)
        grad_normed = lax.optimization_barrier(jnp.sum(rounded(partial_value), axis=3))
        grad_united = grad_normed * gain_values - (grad_rate * row_scale ** 3 / D)[..., None] * united
        gain_grad = lax.optimization_barrier(jnp.sum(grad_normed * united, axis=(1, 2)))
        mix_grad = lax.optimization_barrier(jnp.sum(grad_united * (earlier - floats), axis=(1, 2)))
        below = upstream_float + grad_united * (1.0 - mix_values) + later_rows(grad_united * mix_values, linkage)
        upstream = below.astype(jnp.bfloat16)
        first_list.append((rounded(first_grad[0]) + rounded(first_grad[1])).astype(jnp.bfloat16))
        second_list.append((rounded(second_grad[0]) + rounded(second_grad[1])).astype(jnp.bfloat16))
        gain_list.append(rounded(gain_grad[0]) + rounded(gain_grad[1]))
        mix_list.append(rounded(mix_grad[0]) + rounded(mix_grad[1]))
    grad_in = jnp.stack(first_list[::-1])
    grad_out = jnp.stack(second_list[::-1])
    grad_gain = jnp.stack(gain_list[::-1])
    grad_mix = jnp.stack(mix_list[::-1])
    return (grad_in, grad_out, grad_gain, grad_mix)
```

```python
import functools

import jax
import jax.numpy as jnp
from jax import lax
from jax.experimental import pallas as pl
from jax.experimental.pallas import tpu as pltpu
from jax.sharding import PartitionSpec as P

epsilon = 1e-05
MESH = pl.DeviceIdType.MESH
NT = (((1,), (1,)), ((), ()))
TN = (((0,), (0,)), ((), ()))


def row_linkage(segment_ids):
    joined = segment_ids[..., 1:] == segment_ids[..., :-1]
    leading = jnp.zeros(segment_ids.shape[:-1] + (1,), jnp.float32)
    return jnp.concatenate([leading, joined.astype(jnp.float32)], axis=-1)


def wait_bytes(ref, sem):
    pltpu.make_async_copy(ref, ref, sem).wait()


def relay_kernel(
    n,
    sections,
    entering_ref,
    upstream_ref,
    link_ref,
    gain_ref,
    mix_ref,
    w_in_hbm,
    w_out_hbm,
    normed_ref,
    gate_ref,
    hidden_ref,
    up_ref,
    gain_out,
    mix_out,
    ag,
    part_out,
    part_in,
    sec_in,
    sec_out,
    w_in,
    w_out,
    summed_ref,
    hidden_grad,
    scale_ref,
    rate_out,
    rate_in,
    gain_acc,
    mix_acc,
    ag_send,
    ag_recv,
    rs_send,
    rs_recv,
    rate_send,
    rate_recv,
    sec_send,
    sec_recv,
    w_sem,
):
    me = lax.axis_index("tp")
    sec = lax.axis_index("section")
    micro, rows, width = entering_ref.shape
    tok = rows // 2
    lanes = rate_out.shape[-1]

    def load_in(j):
        return pltpu.make_async_copy(
            w_in_hbm.at[:, pl.ds(pl.multiple_of(j * width, width), width)],
            w_in.at[j],
            w_sem.at[0, j],
        )

    def load_out(j):
        return pltpu.make_async_copy(
            w_out_hbm.at[:, pl.ds(pl.multiple_of(j * width, width), width)],
            w_out.at[j],
            w_sem.at[1, j],
        )

    for j in range(n):
        load_in(j).start()
    for j in range(n):
        load_out(j).start()

    barrier = pltpu.get_barrier_semaphore()

    @pl.loop(1, n)
    def _(d):
        pl.semaphore_signal(
            barrier, inc=1, device_id={"tp": lax.rem(me + d, n)}, device_id_type=MESH
        )

    @pl.when(sec > 0)
    def _():
        pl.semaphore_signal(
            barrier, inc=1, device_id={"section": sec - 1}, device_id_type=MESH
        )

    @pl.when(sec < sections - 1)
    def _():
        pl.semaphore_signal(
            barrier, inc=1, device_id={"section": sec + 1}, device_id_type=MESH
        )

    outer = jnp.logical_or(sec == 0, sec == sections - 1)

    @pl.when(outer)
    def _():
        pl.semaphore_wait(barrier, n)

    @pl.when(jnp.logical_not(outer))
    def _():
        pl.semaphore_wait(barrier, n + 1)

    gain_acc[...] = jnp.zeros_like(gain_acc)
    mix_acc[...] = jnp.zeros_like(mix_acc)

    def gather_copy(phase, m, source, peer):
        return pltpu.make_async_remote_copy(
            src_ref=ag.at[phase, m, source],
            dst_ref=ag.at[phase, m, source],
            send_sem=ag_send.at[phase, m],
            recv_sem=ag_recv.at[phase, m, source],
            device_id={"tp": peer},
            device_id_type=MESH,
        )

    def part_copy(phase, m, peer):
        return pltpu.make_async_remote_copy(
            src_ref=part_out.at[phase, m, peer],
            dst_ref=part_in.at[phase, m, me],
            send_sem=rs_send.at[phase, m],
            recv_sem=rs_recv.at[phase, m],
            device_id={"tp": peer},
            device_id_type=MESH,
        )

    def rate_copy(m, peer):
        return pltpu.make_async_remote_copy(
            src_ref=rate_out.at[m],
            dst_ref=rate_in.at[m, me],
            send_sem=rate_send.at[m],
            recv_sem=rate_recv.at[m],
            device_id={"tp": peer},
            device_id_type=MESH,
        )

    def section_copy(phase, m, target):
        return pltpu.make_async_remote_copy(
            src_ref=sec_out.at[phase, m],
            dst_ref=sec_in.at[phase, m],
            send_sem=sec_send.at[phase, m],
            recv_sem=sec_recv.at[phase, m],
            device_id={"section": target},
            device_id_type=MESH,
        )

    def enter(phase, m, first, start_ref):
        @pl.when(first)
        def _():
            ag[phase, m, me] = start_ref[m]

        @pl.when(jnp.logical_not(first))
        def _():
            section_copy(phase, m, sec).wait_recv()
            ag[phase, m, me] = sec_in[phase, m]

        @pl.loop(1, n)
        def _(d):
            gather_copy(phase, m, me, lax.rem(me + d, n)).start()

    def arrive(phase, m, d):
        source = lax.rem(me - d + n, n)

        @pl.when(d > 0)
        def _():
            gather_copy(phase, m, source, me).wait_recv()

        return source

    def reduced(phase, m):
        wait_bytes(part_in.at[phase, m, pl.ds(0, n - 1)], rs_recv.at[phase, m])
        own = part_out[phase, m, me].astype(jnp.float32)

        def add(d, total):
            return total + part_in[phase, m, lax.rem(me + d, n)].astype(jnp.float32)

        return lax.fori_loop(1, n, add, own)

    def store_rows(ref, m, values):
        start = pl.multiple_of(m * tok, tok)
        for p in range(2):
            ref[p, pl.ds(start, tok), :] = values[p * tok : (p + 1) * tok]

    def mixed(m, source):
        floats = ag[0, m, source].astype(jnp.float32)
        earlier = pltpu.roll(floats, 1, 0) * link_ref[m]
        delta = earlier - floats
        return floats, delta, floats + mix_ref[source] * delta

    def forward(m):
        enter(0, m, sec == 0, entering_ref)
        summed_ref[m] = jnp.zeros_like(summed_ref[m])

        def gather_step(d, squares):
            source = arrive(0, m, d)

            @pl.when(m == 0)
            def _():
                load_in(source).wait()

            _, _, united = mixed(m, source)
            normed = (united * gain_ref[source]).astype(jnp.bfloat16)
            store_rows(normed_ref.at[source], m, normed)
            summed_ref[m] += lax.dot_general(
                normed, w_in[source], NT, preferred_element_type=jnp.float32
            )
            return squares + jnp.sum(united * united, axis=-1, keepdims=True)

        squares = lax.fori_loop(0, n, gather_step, jnp.zeros((rows, 1), jnp.float32))
        row_scale = lax.rsqrt(squares / (n * width) + epsilon)
        scale_ref[m] = jnp.broadcast_to(row_scale, scale_ref.shape[1:])
        pre_act = row_scale * summed_ref[m]
        hidden = (pre_act / (1.0 + jnp.exp(-pre_act))).astype(jnp.bfloat16)
        store_rows(hidden_ref, m, hidden)

        def part(target):
            @pl.when(m == 0)
            def _():
                load_out(target).wait()

            rows_in = jnp.concatenate(
                [hidden_ref[p, pl.ds(pl.multiple_of(m * tok, tok), tok), :] for p in range(2)]
            )
            part_out[0, m, target] = jnp.dot(
                rows_in, w_out[target], preferred_element_type=jnp.float32
            ).astype(jnp.bfloat16)

        @pl.loop(1, n)
        def _(d):
            target = lax.rem(me + d, n)
            part(target)
            part_copy(0, m, target).start()

        part(me)
        below = ag[0, m, me].astype(jnp.float32) + reduced(0, m)
        sec_out[0, m] = below.astype(jnp.bfloat16)

        @pl.when(sec < sections - 1)
        def _():
            section_copy(0, m, sec + 1).start()

    def backward(m):
        enter(1, m, sec == sections - 1, upstream_ref)
        hidden_grad[...] = jnp.zeros_like(hidden_grad)

        @pl.loop(0, n)
        def _(d):
            source = arrive(1, m, d)
            values = ag[1, m, source]
            store_rows(up_ref.at[source], m, values)
            hidden_grad[...] += lax.dot_general(
                values, w_out[source], NT, preferred_element_type=jnp.float32
            )

        row_scale = scale_ref[m][:, :1]
        summed = summed_ref[m]
        pre_act = row_scale * summed
        sigmoid = 1.0 / (1.0 + jnp.exp(-pre_act))
        gate_grad = hidden_grad[...] * (sigmoid * (1.0 + pre_act * (1.0 - sigmoid)))
        store_rows(gate_ref, m, (gate_grad * row_scale).astype(jnp.bfloat16))
        rate = jnp.sum(gate_grad * summed, axis=-1, keepdims=True)
        diagonal = lax.broadcasted_iota(jnp.int32, (rows, lanes), 0) == lax.broadcasted_iota(
            jnp.int32, (rows, lanes), 1
        )
        rate_row = jnp.sum(jnp.where(diagonal, rate, 0.0), axis=0, keepdims=True)
        rate_out[m] = jnp.broadcast_to(rate_row, rate_out.shape[1:])

        @pl.loop(1, n)
        def _(d):
            rate_copy(m, lax.rem(me + d, n)).start()

        def part(target):
            rows_in = jnp.concatenate(
                [gate_ref[p, pl.ds(pl.multiple_of(m * tok, tok), tok), :] for p in range(2)]
            )
            part_out[1, m, target] = jnp.dot(
                rows_in, w_in[target], preferred_element_type=jnp.float32
            ).astype(jnp.bfloat16)

        @pl.loop(1, n)
        def _(d):
            target = lax.rem(me + d, n)
            part(target)
            part_copy(1, m, target).start()

        part(me)
        wait_bytes(rate_in.at[m, pl.ds(0, n - 1)], rate_recv.at[m])

        def add_rate(d, total):
            return total + rate_in[m, lax.rem(me + d, n)]

        rates = lax.fori_loop(1, n, add_rate, rate_out[m])
        grad_rate = jnp.sum(jnp.where(diagonal, rates[:1], 0.0), axis=-1, keepdims=True)
        grad_normed = reduced(1, m)
        _, delta, united = mixed(m, me)
        mix = mix_ref[me]
        factor = grad_rate * (row_scale * row_scale * row_scale) / (n * width)
        grad_united = grad_normed * gain_ref[me] - factor * united
        gain_rows = grad_normed * united
        mix_rows = grad_united * delta
        for p in range(2):
            own = slice(p * tok, (p + 1) * tok)
            gain_acc[p] += jnp.sum(gain_rows[own], axis=0, keepdims=True)
            mix_acc[p] += jnp.sum(mix_rows[own], axis=0, keepdims=True)
        later = pltpu.roll(link_ref[m] * (grad_united * mix), rows - 1, 0)
        below = ag[1, m, me].astype(jnp.float32) + grad_united * (1.0 - mix) + later
        sec_out[1, m] = below.astype(jnp.bfloat16)

        @pl.when(sec > 0)
        def _():
            section_copy(1, m, sec - 1).start()

    @pl.loop(0, micro)
    def _(m):
        forward(m)

    @pl.loop(0, micro)
    def _(m):
        backward(m)

    def twice_rounded(acc):
        return acc[0].astype(jnp.bfloat16).astype(jnp.float32) + acc[1].astype(
            jnp.bfloat16
        ).astype(jnp.float32)

    gain_out[...] = twice_rounded(gain_acc)
    mix_out[...] = twice_rounded(mix_acc)

    @pl.loop(0, micro)
    def _(m):
        for phase in range(2):
            wait_bytes(ag.at[phase, m, pl.ds(0, n - 1)], ag_send.at[phase, m])
            wait_bytes(part_out.at[phase, m, pl.ds(0, n - 1)], rs_send.at[phase, m])
        wait_bytes(rate_in.at[m, pl.ds(0, n - 1)], rate_send.at[m])

        @pl.when(sec < sections - 1)
        def _():
            section_copy(0, m, sec).wait_send()

        @pl.when(sec > 0)
        def _():
            section_copy(1, m, sec).wait_send()


def grads_kernel(normed_ref, gate_ref, hidden_ref, up_ref, grad_in_ref, grad_out_ref):
    def summed(left, right):
        pair = [
            lax.dot_general(left[p], right[p], TN, preferred_element_type=jnp.float32)
            .astype(jnp.bfloat16)
            .astype(jnp.float32)
            for p in range(2)
        ]
        return (pair[0] + pair[1]).astype(jnp.bfloat16)

    grad_in_ref[0] = summed(gate_ref, normed_ref[0])
    grad_out_ref[0] = summed(hidden_ref, up_ref[0])


def local(
    entering, output_grad, live_counts, segment_ids, weight_in, weight_out, norm_gain, shift_mix
):
    sections = lax.axis_size("section")
    n = lax.axis_size("tp")
    relays, micro, tok, width = entering.shape
    rows = relays * tok
    hidden = weight_in.shape[2]
    width_all = weight_in.shape[1]
    lanes = -(-rows // 128) * 128
    linkage = row_linkage(segment_ids)
    live_rows = jnp.arange(tok)[None, None, :] < live_counts[..., None]
    upstream = jnp.where(live_rows[..., None], output_grad, jnp.zeros_like(output_grad))

    def by_micro(values):
        return jnp.swapaxes(values, 0, 1).reshape((micro, rows) + values.shape[3:])

    bf16, f32 = jnp.bfloat16, jnp.float32
    vmem = pl.BlockSpec(memory_space=pltpu.VMEM)
    hbm = pl.BlockSpec(memory_space=pl.ANY)
    dma = pltpu.SemaphoreType.DMA
    normed, gate, hidden_rows, up, gain, mix = pl.pallas_call(
        functools.partial(relay_kernel, n, sections),
        out_shape=(
            jax.ShapeDtypeStruct((n, 2, micro * tok, width), bf16),
            jax.ShapeDtypeStruct((2, micro * tok, hidden), bf16),
            jax.ShapeDtypeStruct((2, micro * tok, hidden), bf16),
            jax.ShapeDtypeStruct((n, 2, micro * tok, width), bf16),
            jax.ShapeDtypeStruct((1, width), f32),
            jax.ShapeDtypeStruct((1, width), f32),
        ),
        in_specs=[vmem] * 5 + [hbm] * 2,
        out_specs=(vmem,) * 6,
        scratch_shapes=[
            pltpu.VMEM((2, micro, n, rows, width), bf16),
            pltpu.VMEM((2, micro, n, rows, width), bf16),
            pltpu.VMEM((2, micro, n, rows, width), bf16),
            pltpu.VMEM((2, micro, rows, width), bf16),
            pltpu.VMEM((2, micro, rows, width), bf16),
            pltpu.VMEM((n, hidden, width), bf16),
            pltpu.VMEM((n, hidden, width), bf16),
            pltpu.VMEM((micro, rows, hidden), f32),
            pltpu.VMEM((rows, hidden), f32),
            pltpu.VMEM((micro, rows, 128), f32),
            pltpu.VMEM((micro, 8, lanes), f32),
            pltpu.VMEM((micro, n, 8, lanes), f32),
            pltpu.VMEM((2, 1, width), f32),
            pltpu.VMEM((2, 1, width), f32),
            dma((2, micro)),
            dma((2, micro, n)),
            dma((2, micro)),
            dma((2, micro)),
            dma((micro,)),
            dma((micro,)),
            dma((2, micro)),
            dma((2, micro)),
            dma((2, n)),
        ],
        compiler_params=pltpu.CompilerParams(
            collective_id=0, has_side_effects=True, vmem_limit_bytes=60 * 1024 * 1024
        ),
        name="relays",
    )(
        by_micro(entering),
        by_micro(upstream),
        by_micro(linkage)[..., None],
        norm_gain[0].astype(f32).reshape(n, 1, width),
        shift_mix[0].astype(f32).reshape(n, 1, width),
        jnp.swapaxes(weight_in[0], 0, 1),
        weight_out[0],
    )

    total = micro * tok
    part = pl.BlockSpec((1, 2, total, width), lambda j: (j, 0, 0, 0))
    whole = pl.BlockSpec((2, total, hidden), lambda j: (0, 0, 0))
    grad_in, grad_out = pl.pallas_call(
        grads_kernel,
        grid=(n,),
        out_shape=(
            jax.ShapeDtypeStruct((1, hidden, width_all), bf16),
            jax.ShapeDtypeStruct((1, hidden, width_all), bf16),
        ),
        in_specs=[part, whole, whole, part],
        out_specs=(
            pl.BlockSpec((1, hidden, width), lambda j: (0, 0, j)),
            pl.BlockSpec((1, hidden, width), lambda j: (0, 0, j)),
        ),
        compiler_params=pltpu.CompilerParams(
            dimension_semantics=("arbitrary",), vmem_limit_bytes=60 * 1024 * 1024
        ),
        name="weight_grads",
    )(normed, gate, hidden_rows, up)
    return jnp.swapaxes(grad_in, 1, 2), grad_out, gain, mix


def solution(mesh):
    in_specs = (
        P(None, None, None, "tp"),
        P(None, None, None, "tp"),
        P(),
        P(),
        P("section", None, "tp"),
        P("section", "tp", None),
        P("section", None),
        P("section", None),
    )
    out_specs = (
        P("section", None, "tp"),
        P("section", "tp", None),
        P("section", "tp"),
        P("section", "tp"),
    )
    return jax.shard_map(local, mesh=mesh, in_specs=in_specs, out_specs=out_specs, check_vma=False)
```

```python
import functools

import jax
import jax.numpy as jnp
from jax import lax
from jax.experimental import pallas as pl
from jax.experimental.pallas import tpu as pltpu
from jax.sharding import PartitionSpec as P

epsilon = 1e-05
MESH = pl.DeviceIdType.MESH
NT = (((1,), (1,)), ((), ()))
TN = (((0,), (0,)), ((), ()))


def wait_bytes(ref, sem):
    pltpu.make_async_copy(ref, ref, sem).wait()


def relay_kernel(
    n,
    sections,
    live_ref,
    entering_ref,
    upstream_ref,
    segment_ref,
    gain_row,
    mix_row,
    w_in_hbm,
    w_out_hbm,
    normed_ref,
    gate_ref,
    hidden_ref,
    up_ref,
    gain_acc,
    mix_acc,
    ag,
    pair_out,
    pair_in,
    part_out,
    part_in,
    sec_out,
    link_ref,
    live_rows,
    gain_ref,
    mix_ref,
    w_in,
    w_out,
    summed_ref,
    hidden_grad,
    scale_ref,
    rate_out,
    rate_in,
    ag_send,
    ag_recv,
    pair_send,
    pair_recv,
    rs_send,
    rs_recv,
    rate_send,
    rate_recv,
    sec_send,
    sec_recv,
    w_sem,
):
    me = lax.axis_index("tp")
    sec = lax.axis_index("section")
    _, micro, tok, width = entering_ref.shape
    rows = 2 * tok
    chips = n // 2
    chip = me // 2
    core = lax.rem(me, 2)
    sibling = me + 1 - 2 * core
    last = sections - 1
    lanes = rate_out.shape[-1]

    def load_in(j):
        return pltpu.make_async_copy(
            w_in_hbm.at[:, pl.ds(pl.multiple_of(j * width, width), width)],
            w_in.at[j],
            w_sem.at[0, j],
        )

    def load_out(j):
        return pltpu.make_async_copy(
            w_out_hbm.at[:, pl.ds(pl.multiple_of(j * width, width), width)],
            w_out.at[j],
            w_sem.at[1, j],
        )

    for j in range(n):
        load_in(j).start()
    for j in range(n):
        load_out(j).start()

    square = [lax.broadcasted_iota(jnp.int32, (tok, tok), axis) for axis in range(2)]
    column = lax.broadcasted_iota(jnp.int32, (tok, 1), 0)
    for p in range(2):
        for m in range(micro):
            own = slice(p * tok, (p + 1) * tok)
            ids = segment_ref[p, m : m + 1, :].astype(jnp.float32)
            here = jnp.sum(jnp.where(square[0] == square[1], ids, 0.0), axis=-1, keepdims=True)
            before = jnp.sum(
                jnp.where(square[0] == square[1] + 1, ids, 0.0), axis=-1, keepdims=True
            )
            joined = jnp.logical_and(here == before, column > 0)
            link_ref[m, own, :] = jnp.where(joined, 1.0, 0.0)
            live_rows[m, own, :] = jnp.where(column < live_ref[p, m], 1.0, 0.0)
    for j in range(n):
        own = slice(j * width, (j + 1) * width)
        gain_ref[j] = gain_row[:, own].astype(jnp.float32)
        mix_ref[j] = mix_row[:, own].astype(jnp.float32)

    barrier = pltpu.get_barrier_semaphore()

    @pl.loop(1, n)
    def _(d):
        pl.semaphore_signal(
            barrier, inc=1, device_id={"tp": lax.rem(me + d, n)}, device_id_type=MESH
        )

    @pl.when(sec > 0)
    def _():
        pl.semaphore_signal(
            barrier, inc=1, device_id={"section": sec - 1}, device_id_type=MESH
        )

    @pl.when(sec < sections - 1)
    def _():
        pl.semaphore_signal(
            barrier, inc=1, device_id={"section": sec + 1}, device_id_type=MESH
        )

    outer = jnp.logical_or(sec == 0, sec == sections - 1)

    @pl.when(outer)
    def _():
        pl.semaphore_wait(barrier, n)

    @pl.when(jnp.logical_not(outer))
    def _():
        pl.semaphore_wait(barrier, n + 1)

    gain_acc[...] = jnp.zeros_like(gain_acc)
    mix_acc[...] = jnp.zeros_like(mix_acc)

    def gather_copy(phase, m, source, peer):
        return pltpu.make_async_remote_copy(
            src_ref=ag.at[phase, m, source],
            dst_ref=ag.at[phase, m, source],
            send_sem=ag_send.at[phase, m],
            recv_sem=ag_recv.at[phase, m, source],
            device_id={"tp": peer},
            device_id_type=MESH,
        )

    def pair_copy(phase, m, target):
        return pltpu.make_async_remote_copy(
            src_ref=pair_out.at[phase, m, target],
            dst_ref=pair_in.at[phase, m, target],
            send_sem=pair_send.at[phase, m],
            recv_sem=pair_recv.at[phase, m, target],
            device_id={"tp": sibling},
            device_id_type=MESH,
        )

    def part_copy(phase, m, target):
        return pltpu.make_async_remote_copy(
            src_ref=part_out.at[phase, m, target],
            dst_ref=part_in.at[phase, m, chip],
            send_sem=rs_send.at[phase, m],
            recv_sem=rs_recv.at[phase, m],
            device_id={"tp": 2 * target + core},
            device_id_type=MESH,
        )

    def rate_copy(m, peer):
        return pltpu.make_async_remote_copy(
            src_ref=rate_out.at[m],
            dst_ref=rate_in.at[m, me],
            send_sem=rate_send.at[m],
            recv_sem=rate_recv.at[m],
            device_id={"tp": peer},
            device_id_type=MESH,
        )

    def section_copy(phase, m, target):
        return pltpu.make_async_remote_copy(
            src_ref=sec_out.at[phase, m],
            dst_ref=ag.at[phase, m, me],
            send_sem=sec_send.at[phase, m],
            recv_sem=sec_recv.at[phase, m],
            device_id={"section": target},
            device_id_type=MESH,
        )

    def spread(phase, m):
        @pl.loop(1, chips)
        def _(k):
            gather_copy(phase, m, me, 2 * lax.rem(chip + k, chips) + core).start()

        gather_copy(phase, m, me, sibling).start()

    def enter_forward(m):
        @pl.when(sec == 0)
        def _():
            for p in range(2):
                ag[0, m, me, p * tok : (p + 1) * tok, :] = entering_ref[p, m]

        @pl.when(sec > 0)
        def _():
            section_copy(0, m, sec).wait_recv()

        spread(0, m)

    def arrive(phase, m, d):
        k = d // 2
        other = lax.rem(d, 2)
        source = 2 * lax.rem(chip - k + chips, chips) + core + other * (1 - 2 * core)

        @pl.when(d > 0)
        def _():
            gather_copy(phase, m, source, me).wait_recv()

        @pl.when(jnp.logical_and(d > 0, other == 0))
        def _():
            gather_copy(phase, m, source, sibling).start()

        return source

    def scatter(phase, m, values_ref, weights):
        start = pl.multiple_of(m * tok, tok)
        values = jnp.concatenate([values_ref[p, pl.ds(start, tok), :] for p in range(2)])
        skew = min(2, chips)

        @pl.loop(0, chips + skew)
        def _(i):
            @pl.when(i < chips)
            def _():
                target = lax.rem(chip + 1 + i, chips)
                pair_out[phase, m, target] = jnp.dot(
                    values,
                    weights[2 * target + 1 - core],
                    preferred_element_type=jnp.float32,
                ).astype(jnp.bfloat16)
                pair_copy(phase, m, target).start()

            @pl.when(i >= skew)
            def _():
                target = lax.rem(chip + 1 + i - skew + chips, chips)
                own = jnp.dot(
                    values, weights[2 * target + core], preferred_element_type=jnp.float32
                )
                pair_copy(phase, m, target).wait_recv()
                part_out[phase, m, target] = (
                    own + pair_in[phase, m, target].astype(jnp.float32)
                ).astype(jnp.bfloat16)

                @pl.when(i < chips + skew - 1)
                def _():
                    part_copy(phase, m, target).start()

    def reduced(phase, m):
        wait_bytes(part_in.at[phase, m, pl.ds(0, chips - 1)], rs_recv.at[phase, m])
        own = part_out[phase, m, chip].astype(jnp.float32)

        def add(k, total):
            return total + part_in[phase, m, lax.rem(chip + k, chips)].astype(jnp.float32)

        return lax.fori_loop(1, chips, add, own)

    def store_rows(ref, m, values):
        start = pl.multiple_of(m * tok, tok)
        for p in range(2):
            ref[p, pl.ds(start, tok), :] = values[p * tok : (p + 1) * tok]

    def mixed(m, source):
        floats = ag[0, m, source].astype(jnp.float32)
        earlier = pltpu.roll(floats, 1, 0) * link_ref[m]
        delta = earlier - floats
        return floats, delta, floats + mix_ref[source] * delta

    def forward(m):
        summed_ref[m] = jnp.zeros_like(summed_ref[m])

        def gather_step(d, squares):
            source = arrive(0, m, d)

            @pl.when(m == 0)
            def _():
                load_in(source).wait()

            _, _, united = mixed(m, source)
            normed = (united * gain_ref[source]).astype(jnp.bfloat16)
            store_rows(normed_ref.at[source], m, normed)
            summed_ref[m] += lax.dot_general(
                normed, w_in[source], NT, preferred_element_type=jnp.float32
            )
            return squares + jnp.sum(united * united, axis=-1, keepdims=True)

        squares = lax.fori_loop(0, n, gather_step, jnp.zeros((rows, 1), jnp.float32))
        row_scale = lax.rsqrt(squares / (n * width) + epsilon)
        scale_ref[m] = jnp.broadcast_to(row_scale, scale_ref.shape[1:])
        pre_act = row_scale * summed_ref[m]
        hidden = (pre_act / (1.0 + jnp.exp(-pre_act))).astype(jnp.bfloat16)
        store_rows(hidden_ref, m, hidden)

        @pl.when(m == 0)
        def _():
            for j in range(n):
                load_out(j).wait()

        @pl.when(sec < last)
        def _():
            scatter(0, m, hidden_ref, w_out)

    def finish_forward(m):
        below = ag[0, m, me].astype(jnp.float32) + reduced(0, m)
        sec_out[0, m] = below.astype(jnp.bfloat16)
        section_copy(0, m, sec + 1).start()

    def enter_backward(m):
        @pl.when(sec == last)
        def _():
            for p in range(2):
                own = slice(p * tok, (p + 1) * tok)
                ag[1, m, me, own, :] = (
                    upstream_ref[p, m].astype(jnp.float32) * live_rows[m, own, :]
                ).astype(jnp.bfloat16)

        @pl.when(sec < last)
        def _():
            section_copy(1, m, sec).wait_recv()

        spread(1, m)

    diagonal = lax.broadcasted_iota(jnp.int32, (rows, lanes), 0) == lax.broadcasted_iota(
        jnp.int32, (rows, lanes), 1
    )

    def backward(m):
        hidden_grad[...] = jnp.zeros_like(hidden_grad)

        @pl.loop(0, n)
        def _(d):
            source = arrive(1, m, d)
            values = ag[1, m, source]
            store_rows(up_ref.at[source], m, values)
            hidden_grad[...] += lax.dot_general(
                values, w_out[source], NT, preferred_element_type=jnp.float32
            )

        row_scale = scale_ref[m][:, :1]
        summed = summed_ref[m]
        pre_act = row_scale * summed
        sigmoid = 1.0 / (1.0 + jnp.exp(-pre_act))
        gate_grad = hidden_grad[...] * (sigmoid * (1.0 + pre_act * (1.0 - sigmoid)))
        store_rows(gate_ref, m, (gate_grad * row_scale).astype(jnp.bfloat16))
        rate = jnp.sum(gate_grad * summed, axis=-1, keepdims=True)
        rate_row = jnp.sum(jnp.where(diagonal, rate, 0.0), axis=0, keepdims=True)
        rate_out[m] = jnp.broadcast_to(rate_row, rate_out.shape[1:])

        @pl.loop(1, n)
        def _(d):
            rate_copy(m, lax.rem(me + d, n)).start()

        scatter(1, m, gate_ref, w_in)

    def finish_backward(m):
        row_scale = scale_ref[m][:, :1]
        wait_bytes(rate_in.at[m, pl.ds(0, n - 1)], rate_recv.at[m])

        def add_rate(d, total):
            return total + rate_in[m, lax.rem(me + d, n)]

        rates = lax.fori_loop(1, n, add_rate, rate_out[m])
        grad_rate = jnp.sum(jnp.where(diagonal, rates[:1], 0.0), axis=-1, keepdims=True)
        grad_normed = reduced(1, m)
        _, delta, united = mixed(m, me)
        mix = mix_ref[me]
        factor = grad_rate * (row_scale * row_scale * row_scale) / (n * width)
        grad_united = grad_normed * gain_ref[me] - factor * united
        gain_rows = grad_normed * united
        mix_rows = grad_united * delta
        for p in range(2):
            own = slice(p * tok, (p + 1) * tok)
            gain_acc[p] += jnp.sum(gain_rows[own], axis=0, keepdims=True)
            mix_acc[p] += jnp.sum(mix_rows[own], axis=0, keepdims=True)
        later = pltpu.roll(link_ref[m] * (grad_united * mix), rows - 1, 0)
        below = ag[1, m, me].astype(jnp.float32) + grad_united * (1.0 - mix) + later
        sec_out[1, m] = below.astype(jnp.bfloat16)

        @pl.when(sec > 0)
        def _():
            section_copy(1, m, sec - 1).start()

    enter_forward(0)

    @pl.when(sec == last)
    def _():
        @pl.loop(0, micro)
        def _(m):
            enter_backward(m)

    @pl.loop(0, micro)
    def _(m):
        forward(m)

        @pl.when(m < micro - 1)
        def _():
            enter_forward(m + 1)

        @pl.when(sec < last)
        def _():
            finish_forward(m)

    @pl.when(sec < last)
    def _():
        enter_backward(0)

    @pl.loop(0, micro)
    def _(m):
        backward(m)

        @pl.when(jnp.logical_and(m < micro - 1, sec < last))
        def _():
            enter_backward(m + 1)

        finish_backward(m)

    @pl.loop(0, micro)
    def _(m):
        def sent(phase):
            wait_bytes(pair_out.at[phase, m], pair_send.at[phase, m])
            wait_bytes(part_out.at[phase, m, pl.ds(0, chips - 1)], rs_send.at[phase, m])

        for phase in range(2):
            wait_bytes(ag.at[phase, m, pl.ds(0, n - 1)], ag_send.at[phase, m])
        sent(1)
        wait_bytes(rate_in.at[m, pl.ds(0, n - 1)], rate_send.at[m])

        @pl.when(sec < last)
        def _():
            sent(0)
            section_copy(0, m, sec).wait_send()

        @pl.when(sec > 0)
        def _():
            section_copy(1, m, sec).wait_send()


def grads_kernel(
    normed_ref, gate_ref, hidden_ref, up_ref, gain_ref, mix_ref, grad_in, grad_out, gain, mix
):
    def summed(left, right):
        left, right = [v.reshape((-1, v.shape[-1])) for v in (left, right)]
        return lax.dot_general(left, right, TN, preferred_element_type=jnp.float32)

    def twice_rounded(acc):
        pair = [acc[p].astype(jnp.bfloat16).astype(jnp.float32) for p in range(2)]
        return pair[0] + pair[1]

    grad_in[0] = summed(gate_ref[...], normed_ref[0]).astype(grad_in.dtype)
    grad_out[0] = summed(hidden_ref[...], up_ref[0]).astype(grad_out.dtype)
    gain[...] = twice_rounded(gain_ref)
    mix[...] = twice_rounded(mix_ref)


def local(
    entering, output_grad, live_counts, segment_ids, weight_in, weight_out, norm_gain, shift_mix
):
    sections = lax.axis_size("section")
    n = lax.axis_size("tp")
    relays, micro, tok, width = entering.shape
    rows = relays * tok
    hidden = weight_in.shape[2]
    width_all = weight_in.shape[1]
    lanes = -(-rows // 128) * 128
    bf16, f32 = jnp.bfloat16, jnp.float32
    vmem = pl.BlockSpec(memory_space=pltpu.VMEM)
    smem = pl.BlockSpec(memory_space=pltpu.SMEM)
    hbm = pl.BlockSpec(memory_space=pl.ANY)
    dma = pltpu.SemaphoreType.DMA
    normed, gate, hidden_rows, up, gain_sums, mix_sums = pl.pallas_call(
        functools.partial(relay_kernel, n, sections),
        out_shape=(
            jax.ShapeDtypeStruct((n, 2, micro * tok, width), bf16),
            jax.ShapeDtypeStruct((2, micro * tok, hidden), bf16),
            jax.ShapeDtypeStruct((2, micro * tok, hidden), bf16),
            jax.ShapeDtypeStruct((n, 2, micro * tok, width), bf16),
            jax.ShapeDtypeStruct((2, 1, width), f32),
            jax.ShapeDtypeStruct((2, 1, width), f32),
        ),
        in_specs=[smem] + [vmem] * 5 + [hbm] * 2,
        out_specs=(vmem,) * 6,
        scratch_shapes=[
            pltpu.VMEM((2, micro, n, rows, width), bf16),
            pltpu.VMEM((2, micro, n // 2, rows, width), bf16),
            pltpu.VMEM((2, micro, n // 2, rows, width), bf16),
            pltpu.VMEM((2, micro, n // 2, rows, width), bf16),
            pltpu.VMEM((2, micro, n // 2, rows, width), bf16),
            pltpu.VMEM((2, micro, rows, width), bf16),
            pltpu.VMEM((micro, rows, 1), f32),
            pltpu.VMEM((micro, rows, 1), f32),
            pltpu.VMEM((n, 1, width), f32),
            pltpu.VMEM((n, 1, width), f32),
            pltpu.VMEM((n, hidden, width), bf16),
            pltpu.VMEM((n, hidden, width), bf16),
            pltpu.VMEM((micro, rows, hidden), f32),
            pltpu.VMEM((rows, hidden), f32),
            pltpu.VMEM((micro, rows, 128), f32),
            pltpu.VMEM((micro, 8, lanes), f32),
            pltpu.VMEM((micro, n, 8, lanes), f32),
            dma((2, micro)),
            dma((2, micro, n)),
            dma((2, micro)),
            dma((2, micro, n // 2)),
            dma((2, micro)),
            dma((2, micro)),
            dma((micro,)),
            dma((micro,)),
            dma((2, micro)),
            dma((2, micro)),
            dma((2, n)),
        ],
        compiler_params=pltpu.CompilerParams(
            collective_id=0, has_side_effects=True, vmem_limit_bytes=60 * 1024 * 1024
        ),
        name="relays",
    )(
        live_counts,
        entering,
        output_grad,
        segment_ids,
        norm_gain,
        shift_mix,
        jnp.swapaxes(weight_in[0], 0, 1),
        weight_out[0],
    )

    total = micro * tok
    part = pl.BlockSpec((1, 2, total, width), lambda j: (j, 0, 0, 0))
    whole = pl.BlockSpec((2, total, hidden), lambda j: (0, 0, 0))
    sums = pl.BlockSpec((2, 1, width), lambda j: (0, 0, 0))
    row = pl.BlockSpec((1, width), lambda j: (0, 0))
    grad_in, grad_out, gain, mix = pl.pallas_call(
        grads_kernel,
        grid=(n,),
        out_shape=(
            jax.ShapeDtypeStruct((1, hidden, width_all), bf16),
            jax.ShapeDtypeStruct((1, hidden, width_all), bf16),
            jax.ShapeDtypeStruct((1, width), f32),
            jax.ShapeDtypeStruct((1, width), f32),
        ),
        in_specs=[part, whole, whole, part, sums, sums],
        out_specs=(
            pl.BlockSpec((1, hidden, width), lambda j: (0, 0, j)),
            pl.BlockSpec((1, hidden, width), lambda j: (0, 0, j)),
            row,
            row,
        ),
        compiler_params=pltpu.CompilerParams(
            dimension_semantics=("arbitrary",), vmem_limit_bytes=60 * 1024 * 1024
        ),
        name="weight_grads",
    )(normed, gate, hidden_rows, up, gain_sums, mix_sums)
    return jnp.swapaxes(grad_in, 1, 2), grad_out, gain, mix


def solution(mesh):
    in_specs = (
        P(None, None, None, "tp"),
        P(None, None, None, "tp"),
        P(),
        P(),
        P("section", None, "tp"),
        P("section", "tp", None),
        P("section", None),
        P("section", None),
    )
    out_specs = (
        P("section", None, "tp"),
        P("section", "tp", None),
        P("section", "tp"),
        P("section", "tp"),
    )
    return jax.shard_map(local, mesh=mesh, in_specs=in_specs, out_specs=out_specs, check_vma=False)
```

```python
import functools

import jax
import jax.numpy as jnp
from jax import lax
from jax.experimental import pallas as pl
from jax.experimental.pallas import tpu as pltpu
from jax.sharding import PartitionSpec as P

epsilon = 1e-05
MESH = pl.DeviceIdType.MESH
NT = (((1,), (1,)), ((), ()))
TN = (((0,), (0,)), ((), ()))


def wait_bytes(ref, sem):
    pltpu.make_async_copy(ref, ref, sem).wait()


def relay_kernel(
    n,
    sections,
    live_ref,
    entering_ref,
    upstream_ref,
    segment_ref,
    gain_row,
    mix_row,
    w_in_hbm,
    w_out_hbm,
    normed_ref,
    gate_ref,
    hidden_ref,
    up_ref,
    gain_acc,
    mix_acc,
    ag,
    pair_out,
    pair_in,
    part_out,
    part_in,
    sec_out,
    link_ref,
    live_rows,
    gain_ref,
    mix_ref,
    w_in,
    w_out,
    summed_ref,
    hidden_grad,
    scale_ref,
    rate_out,
    rate_in,
    ag_send,
    ag_recv,
    pair_send,
    pair_recv,
    rs_send,
    rs_recv,
    rate_send,
    rate_recv,
    sec_send,
    sec_recv,
    w_sem,
):
    me = lax.axis_index("tp")
    sec = lax.axis_index("section")
    _, micro, tok, width = entering_ref.shape
    rows = 2 * tok
    chips = n // 2
    chip = me // 2
    core = lax.rem(me, 2)
    sibling = me + 1 - 2 * core
    last = sections - 1
    lanes = rate_out.shape[-1]

    def load_in(j):
        return pltpu.make_async_copy(
            w_in_hbm.at[:, pl.ds(pl.multiple_of(j * width, width), width)],
            w_in.at[j],
            w_sem.at[0, j],
        )

    def load_out(j):
        return pltpu.make_async_copy(
            w_out_hbm.at[:, pl.ds(pl.multiple_of(j * width, width), width)],
            w_out.at[j],
            w_sem.at[1, j],
        )

    for j in range(n):
        load_in(j).start()
    for j in range(n):
        load_out(j).start()

    square = [lax.broadcasted_iota(jnp.int32, (tok, tok), axis) for axis in range(2)]
    column = lax.broadcasted_iota(jnp.int32, (tok, 1), 0)
    for p in range(2):
        for m in range(micro):
            own = slice(p * tok, (p + 1) * tok)
            ids = segment_ref[p, m : m + 1, :].astype(jnp.float32)
            here = jnp.sum(jnp.where(square[0] == square[1], ids, 0.0), axis=-1, keepdims=True)
            before = jnp.sum(
                jnp.where(square[0] == square[1] + 1, ids, 0.0), axis=-1, keepdims=True
            )
            joined = jnp.logical_and(here == before, column > 0)
            link_ref[m, own, :] = jnp.where(joined, 1.0, 0.0)
            live_rows[m, own, :] = jnp.where(column < live_ref[p, m], 1.0, 0.0)
    for j in range(n):
        own = slice(j * width, (j + 1) * width)
        gain_ref[j] = gain_row[:, own].astype(jnp.float32)
        mix_ref[j] = mix_row[:, own].astype(jnp.float32)

    barrier = pltpu.get_barrier_semaphore()

    @pl.loop(1, n)
    def _(d):
        pl.semaphore_signal(
            barrier, inc=1, device_id={"tp": lax.rem(me + d, n)}, device_id_type=MESH
        )

    @pl.when(sec > 0)
    def _():
        pl.semaphore_signal(
            barrier, inc=1, device_id={"section": sec - 1}, device_id_type=MESH
        )

    @pl.when(sec < sections - 1)
    def _():
        pl.semaphore_signal(
            barrier, inc=1, device_id={"section": sec + 1}, device_id_type=MESH
        )

    outer = jnp.logical_or(sec == 0, sec == sections - 1)

    @pl.when(outer)
    def _():
        pl.semaphore_wait(barrier, n)

    @pl.when(jnp.logical_not(outer))
    def _():
        pl.semaphore_wait(barrier, n + 1)

    gain_acc[...] = jnp.zeros_like(gain_acc)
    mix_acc[...] = jnp.zeros_like(mix_acc)

    def gather_copy(phase, m, source, peer):
        return pltpu.make_async_remote_copy(
            src_ref=ag.at[phase, m, source],
            dst_ref=ag.at[phase, m, source],
            send_sem=ag_send.at[phase, m],
            recv_sem=ag_recv.at[phase, m, source],
            device_id={"tp": peer},
            device_id_type=MESH,
        )

    def pair_copy(phase, m, target):
        return pltpu.make_async_remote_copy(
            src_ref=pair_out.at[phase, m, target],
            dst_ref=pair_in.at[phase, m, target],
            send_sem=pair_send.at[phase, m],
            recv_sem=pair_recv.at[phase, m, target],
            device_id={"tp": sibling},
            device_id_type=MESH,
        )

    def part_copy(phase, m, target):
        return pltpu.make_async_remote_copy(
            src_ref=part_out.at[phase, m, target],
            dst_ref=part_in.at[phase, m, chip],
            send_sem=rs_send.at[phase, m],
            recv_sem=rs_recv.at[phase, m],
            device_id={"tp": 2 * target + core},
            device_id_type=MESH,
        )

    def rate_copy(m, peer):
        return pltpu.make_async_remote_copy(
            src_ref=rate_out.at[m],
            dst_ref=rate_in.at[m, me],
            send_sem=rate_send.at[m],
            recv_sem=rate_recv.at[m],
            device_id={"tp": peer},
            device_id_type=MESH,
        )

    def section_copy(phase, m, target):
        return pltpu.make_async_remote_copy(
            src_ref=sec_out.at[phase, m],
            dst_ref=ag.at[phase, m, me],
            send_sem=sec_send.at[phase, m],
            recv_sem=sec_recv.at[phase, m],
            device_id={"section": target},
            device_id_type=MESH,
        )

    def spread(phase, m):
        @pl.loop(1, chips)
        def _(k):
            gather_copy(phase, m, me, 2 * lax.rem(chip + k, chips) + core).start()

        gather_copy(phase, m, me, sibling).start()

    def enter_forward(m):
        @pl.when(sec == 0)
        def _():
            for p in range(2):
                ag[0, m, me, p * tok : (p + 1) * tok, :] = entering_ref[p, m]

        @pl.when(sec > 0)
        def _():
            section_copy(0, m, sec).wait_recv()

        spread(0, m)

    def arrive(phase, m, d):
        k = d // 2
        other = lax.rem(d, 2)
        source = 2 * lax.rem(chip - k + chips, chips) + core + other * (1 - 2 * core)

        @pl.when(d > 0)
        def _():
            gather_copy(phase, m, source, me).wait_recv()

        @pl.when(jnp.logical_and(d > 0, other == 0))
        def _():
            gather_copy(phase, m, source, sibling).start()

        return source

    def scatter(phase, m, values_ref, weights):
        start = pl.multiple_of(m * tok, tok)
        values = jnp.concatenate([values_ref[p, pl.ds(start, tok), :] for p in range(2)])
        skew = min(2, chips)

        @pl.loop(0, chips + skew)
        def _(i):
            @pl.when(i < chips)
            def _():
                target = lax.rem(chip + 1 + i, chips)
                pair_out[phase, m, target] = jnp.dot(
                    values,
                    weights[2 * target + 1 - core],
                    preferred_element_type=jnp.float32,
                ).astype(jnp.bfloat16)
                pair_copy(phase, m, target).start()

            @pl.when(i >= skew)
            def _():
                target = lax.rem(chip + 1 + i - skew + chips, chips)
                own = jnp.dot(
                    values, weights[2 * target + core], preferred_element_type=jnp.float32
                )
                pair_copy(phase, m, target).wait_recv()
                part_out[phase, m, target] = (
                    own + pair_in[phase, m, target].astype(jnp.float32)
                ).astype(jnp.bfloat16)

                @pl.when(i < chips + skew - 1)
                def _():
                    part_copy(phase, m, target).start()

    def reduced(phase, m):
        wait_bytes(part_in.at[phase, m, pl.ds(0, chips - 1)], rs_recv.at[phase, m])
        own = part_out[phase, m, chip].astype(jnp.float32)

        def add(k, total):
            return total + part_in[phase, m, lax.rem(chip + k, chips)].astype(jnp.float32)

        return lax.fori_loop(1, chips, add, own)

    def store_rows(ref, m, values):
        start = pl.multiple_of(m * tok, tok)
        for p in range(2):
            ref[p, pl.ds(start, tok), :] = values[p * tok : (p + 1) * tok]

    def mixed(m, source):
        floats = ag[0, m, source].astype(jnp.float32)
        earlier = pltpu.roll(floats, 1, 0) * link_ref[m]
        delta = earlier - floats
        return floats, delta, floats + mix_ref[source] * delta

    def forward(m):
        summed_ref[m] = jnp.zeros_like(summed_ref[m])

        def gather_step(d, squares):
            source = arrive(0, m, d)

            @pl.when(m == 0)
            def _():
                load_in(source).wait()

            _, _, united = mixed(m, source)
            normed = (united * gain_ref[source]).astype(jnp.bfloat16)
            store_rows(normed_ref.at[source], m, normed)
            summed_ref[m] += lax.dot_general(
                normed, w_in[source], NT, preferred_element_type=jnp.float32
            )
            return squares + jnp.sum(united * united, axis=-1, keepdims=True)

        squares = lax.fori_loop(0, n, gather_step, jnp.zeros((rows, 1), jnp.float32))
        row_scale = lax.rsqrt(squares / (n * width) + epsilon)
        scale_ref[m] = jnp.broadcast_to(row_scale, scale_ref.shape[1:])
        pre_act = row_scale * summed_ref[m]
        hidden = (pre_act / (1.0 + jnp.exp(-pre_act))).astype(jnp.bfloat16)
        store_rows(hidden_ref, m, hidden)

        @pl.when(jnp.logical_and(m == 0, sec < last))
        def _():
            for j in range(n):
                load_out(j).wait()

        @pl.when(sec < last)
        def _():
            scatter(0, m, hidden_ref, w_out)

    def finish_forward(m):
        below = ag[0, m, me].astype(jnp.float32) + reduced(0, m)
        sec_out[0, m] = below.astype(jnp.bfloat16)
        section_copy(0, m, sec + 1).start()

    def enter_backward(m):
        @pl.when(sec == last)
        def _():
            for p in range(2):
                own = slice(p * tok, (p + 1) * tok)
                ag[1, m, me, own, :] = (
                    upstream_ref[p, m].astype(jnp.float32) * live_rows[m, own, :]
                ).astype(jnp.bfloat16)

        @pl.when(sec < last)
        def _():
            section_copy(1, m, sec).wait_recv()

        spread(1, m)

    diagonal = lax.broadcasted_iota(jnp.int32, (rows, lanes), 0) == lax.broadcasted_iota(
        jnp.int32, (rows, lanes), 1
    )

    def gather_backward(m):
        hidden_grad[m] = jnp.zeros_like(hidden_grad[m])

        @pl.loop(0, n)
        def _(d):
            source = arrive(1, m, d)
            values = ag[1, m, source]
            store_rows(up_ref.at[source], m, values)
            hidden_grad[m] += lax.dot_general(
                values, w_out[source], NT, preferred_element_type=jnp.float32
            )

    def backward(m):

        row_scale = scale_ref[m][:, :1]
        summed = summed_ref[m]
        pre_act = row_scale * summed
        sigmoid = 1.0 / (1.0 + jnp.exp(-pre_act))
        gate_grad = hidden_grad[m] * (sigmoid * (1.0 + pre_act * (1.0 - sigmoid)))
        store_rows(gate_ref, m, (gate_grad * row_scale).astype(jnp.bfloat16))
        rate = jnp.sum(gate_grad * summed, axis=-1, keepdims=True)
        rate_row = jnp.sum(jnp.where(diagonal, rate, 0.0), axis=0, keepdims=True)
        rate_out[m] = jnp.broadcast_to(rate_row, rate_out.shape[1:])

        @pl.loop(1, n)
        def _(d):
            rate_copy(m, lax.rem(me + d, n)).start()

        scatter(1, m, gate_ref, w_in)

    def finish_backward(m):
        row_scale = scale_ref[m][:, :1]
        wait_bytes(rate_in.at[m, pl.ds(0, n - 1)], rate_recv.at[m])

        def add_rate(d, total):
            return total + rate_in[m, lax.rem(me + d, n)]

        rates = lax.fori_loop(1, n, add_rate, rate_out[m])
        grad_rate = jnp.sum(jnp.where(diagonal, rates[:1], 0.0), axis=-1, keepdims=True)
        grad_normed = reduced(1, m)
        _, delta, united = mixed(m, me)
        mix = mix_ref[me]
        factor = grad_rate * (row_scale * row_scale * row_scale) / (n * width)
        grad_united = grad_normed * gain_ref[me] - factor * united
        gain_rows = grad_normed * united
        mix_rows = grad_united * delta
        for p in range(2):
            own = slice(p * tok, (p + 1) * tok)
            gain_acc[p] += jnp.sum(gain_rows[own], axis=0, keepdims=True)
            mix_acc[p] += jnp.sum(mix_rows[own], axis=0, keepdims=True)
        later = pltpu.roll(link_ref[m] * (grad_united * mix), rows - 1, 0)
        below = ag[1, m, me].astype(jnp.float32) + grad_united * (1.0 - mix) + later
        sec_out[1, m] = below.astype(jnp.bfloat16)

        @pl.when(sec > 0)
        def _():
            section_copy(1, m, sec - 1).start()

    enter_forward(0)

    @pl.when(sec == last)
    def _():
        @pl.loop(0, micro)
        def _(m):
            enter_backward(m)

        for j in range(n):
            load_out(j).wait()

        @pl.loop(0, micro)
        def _(m):
            gather_backward(m)

    @pl.loop(0, micro)
    def _(m):
        forward(m)

        @pl.when(m < micro - 1)
        def _():
            enter_forward(m + 1)

        @pl.when(sec < last)
        def _():
            finish_forward(m)

    @pl.when(sec < last)
    def _():
        enter_backward(0)

    @pl.loop(0, micro)
    def _(m):
        @pl.when(sec < last)
        def _():
            gather_backward(m)

        backward(m)

        @pl.when(jnp.logical_and(m < micro - 1, sec < last))
        def _():
            enter_backward(m + 1)

        finish_backward(m)

    @pl.loop(0, micro)
    def _(m):
        def sent(phase):
            wait_bytes(pair_out.at[phase, m], pair_send.at[phase, m])
            wait_bytes(part_out.at[phase, m, pl.ds(0, chips - 1)], rs_send.at[phase, m])

        for phase in range(2):
            wait_bytes(ag.at[phase, m, pl.ds(0, n - 1)], ag_send.at[phase, m])
        sent(1)
        wait_bytes(rate_in.at[m, pl.ds(0, n - 1)], rate_send.at[m])

        @pl.when(sec < last)
        def _():
            sent(0)
            section_copy(0, m, sec).wait_send()

        @pl.when(sec > 0)
        def _():
            section_copy(1, m, sec).wait_send()


def grads_kernel(
    normed_ref, gate_ref, hidden_ref, up_ref, gain_ref, mix_ref, grad_in, grad_out, gain, mix
):
    def summed(left, right):
        left, right = [v.reshape((-1, v.shape[-1])) for v in (left, right)]
        return lax.dot_general(left, right, TN, preferred_element_type=jnp.float32)

    def twice_rounded(acc):
        pair = [acc[p].astype(jnp.bfloat16).astype(jnp.float32) for p in range(2)]
        return pair[0] + pair[1]

    grad_in[0] = summed(gate_ref[...], normed_ref[0]).astype(grad_in.dtype)
    grad_out[0] = summed(hidden_ref[...], up_ref[0]).astype(grad_out.dtype)
    gain[...] = twice_rounded(gain_ref)
    mix[...] = twice_rounded(mix_ref)


def local(
    entering, output_grad, live_counts, segment_ids, weight_in, weight_out, norm_gain, shift_mix
):
    sections = lax.axis_size("section")
    n = lax.axis_size("tp")
    relays, micro, tok, width = entering.shape
    rows = relays * tok
    hidden = weight_in.shape[2]
    width_all = weight_in.shape[1]
    lanes = -(-rows // 128) * 128
    bf16, f32 = jnp.bfloat16, jnp.float32
    vmem = pl.BlockSpec(memory_space=pltpu.VMEM)
    smem = pl.BlockSpec(memory_space=pltpu.SMEM)
    hbm = pl.BlockSpec(memory_space=pl.ANY)
    dma = pltpu.SemaphoreType.DMA
    normed, gate, hidden_rows, up, gain_sums, mix_sums = pl.pallas_call(
        functools.partial(relay_kernel, n, sections),
        out_shape=(
            jax.ShapeDtypeStruct((n, 2, micro * tok, width), bf16),
            jax.ShapeDtypeStruct((2, micro * tok, hidden), bf16),
            jax.ShapeDtypeStruct((2, micro * tok, hidden), bf16),
            jax.ShapeDtypeStruct((n, 2, micro * tok, width), bf16),
            jax.ShapeDtypeStruct((2, 1, width), f32),
            jax.ShapeDtypeStruct((2, 1, width), f32),
        ),
        in_specs=[smem] + [vmem] * 5 + [hbm] * 2,
        out_specs=(vmem,) * 6,
        scratch_shapes=[
            pltpu.VMEM((2, micro, n, rows, width), bf16),
            pltpu.VMEM((2, micro, n // 2, rows, width), bf16),
            pltpu.VMEM((2, micro, n // 2, rows, width), bf16),
            pltpu.VMEM((2, micro, n // 2, rows, width), bf16),
            pltpu.VMEM((2, micro, n // 2, rows, width), bf16),
            pltpu.VMEM((2, micro, rows, width), bf16),
            pltpu.VMEM((micro, rows, 1), f32),
            pltpu.VMEM((micro, rows, 1), f32),
            pltpu.VMEM((n, 1, width), f32),
            pltpu.VMEM((n, 1, width), f32),
            pltpu.VMEM((n, hidden, width), bf16),
            pltpu.VMEM((n, hidden, width), bf16),
            pltpu.VMEM((micro, rows, hidden), f32),
            pltpu.VMEM((micro, rows, hidden), f32),
            pltpu.VMEM((micro, rows, 128), f32),
            pltpu.VMEM((micro, 8, lanes), f32),
            pltpu.VMEM((micro, n, 8, lanes), f32),
            dma((2, micro)),
            dma((2, micro, n)),
            dma((2, micro)),
            dma((2, micro, n // 2)),
            dma((2, micro)),
            dma((2, micro)),
            dma((micro,)),
            dma((micro,)),
            dma((2, micro)),
            dma((2, micro)),
            dma((2, n)),
        ],
        compiler_params=pltpu.CompilerParams(
            collective_id=0, has_side_effects=True, vmem_limit_bytes=60 * 1024 * 1024
        ),
        name="relays",
    )(
        live_counts,
        entering,
        output_grad,
        segment_ids,
        norm_gain,
        shift_mix,
        jnp.swapaxes(weight_in[0], 0, 1),
        weight_out[0],
    )

    total = micro * tok
    part = pl.BlockSpec((1, 2, total, width), lambda j: (j, 0, 0, 0))
    whole = pl.BlockSpec((2, total, hidden), lambda j: (0, 0, 0))
    sums = pl.BlockSpec((2, 1, width), lambda j: (0, 0, 0))
    row = pl.BlockSpec((1, width), lambda j: (0, 0))
    grad_in, grad_out, gain, mix = pl.pallas_call(
        grads_kernel,
        grid=(n,),
        out_shape=(
            jax.ShapeDtypeStruct((1, hidden, width_all), bf16),
            jax.ShapeDtypeStruct((1, hidden, width_all), bf16),
            jax.ShapeDtypeStruct((1, width), f32),
            jax.ShapeDtypeStruct((1, width), f32),
        ),
        in_specs=[part, whole, whole, part, sums, sums],
        out_specs=(
            pl.BlockSpec((1, hidden, width), lambda j: (0, 0, j)),
            pl.BlockSpec((1, hidden, width), lambda j: (0, 0, j)),
            row,
            row,
        ),
        compiler_params=pltpu.CompilerParams(
            dimension_semantics=("arbitrary",), vmem_limit_bytes=60 * 1024 * 1024
        ),
        name="weight_grads",
    )(normed, gate, hidden_rows, up, gain_sums, mix_sums)
    return jnp.swapaxes(grad_in, 1, 2), grad_out, gain, mix


def solution(mesh):
    in_specs = (
        P(None, None, None, "tp"),
        P(None, None, None, "tp"),
        P(),
        P(),
        P("section", None, "tp"),
        P("section", "tp", None),
        P("section", None),
        P("section", None),
    )
    out_specs = (
        P("section", None, "tp"),
        P("section", "tp", None),
        P("section", "tp"),
        P("section", "tp"),
    )
    return jax.shard_map(local, mesh=mesh, in_specs=in_specs, out_specs=out_specs, check_vma=False)
```
